32 devices in a mesh: ctx: 16 (over z, y, core), mp: 2 (over x).
Axes of the slice: x: 2, y: 2, z: 4, core: 2. Of those that a mesh axis runs over, the one named last changes fastest.
Arguments:
- features: bfloat16 [3, 8192, 4096], P(None, 'ctx', 'mp'), may hold values from -6 to 6
- short_filter: float32 [3, 7, 4096], P(None, None, 'mp'), may hold values from -2 to 2
- residues: float32 [4096, 16], P('mp'), may hold values from -1.5 to 1.5
- rates: float32 [4096, 16], P('mp'), as said below
- out_weight: bfloat16 [4096, 4096], P('ctx', 'mp'), may hold values from -0.125 to 0.125
Outputs:
- mixed: bfloat16 [8192, 4096], P('ctx', 'mp')
The draws below stay inside these ranges and needn't reach their ends.
Inputs may be any that keep to these rules, and one draw needn't show every extreme that they name: `rates`: every rate lies between 0.3 / 8192 and 0.08.
All inputs are finite; a program needn't handle non-finite values.
Results may differ from the reference program's by a relative error of at most 0.0058.
Values may be sent and summed in bfloat16 or wider, within the bound.
A program may use at most 128 MiB of HBM per device.

```python
import math
import jax
import jax.numpy as jnp
from jax import lax

D = 4096
MODES = 16
KERNEL = 7
BLOCK = 128
TOKENS = 8192


def draw_rates(key, part):
    pick_key, slow_key, fast_key = jax.random.split(key, 3)
    slow_rates = jnp.exp(jax.random.uniform(slow_key, (D, MODES), jnp.float32, math.log(0.3 / TOKENS), math.log(2.0 / TOKENS)))
    fast_rates = jnp.exp(jax.random.uniform(fast_key, (D, MODES), jnp.float32, math.log(0.05), math.log(0.08)))
    share = 0.5
    chosen = jax.random.uniform(pick_key, (D, MODES), jnp.float32) < share
    return jnp.where(chosen, slow_rates, fast_rates).astype(jnp.float32)


def with_spikes(values, key, source, target, shards_of, factor):
    owner, partner = [(jnp.arange(values.shape[axis_at]) // (values.shape[axis_at] // shards_of)).reshape([-1 if axis == axis_at else 1 for axis in range(values.ndim)]) for axis_at in (source, target)]
    chosen = jax.random.permutation(key, shards_of)[partner]
    strong = (owner == chosen) | (owner == (partner + shards_of // 2) % shards_of)
    return jnp.where(strong, factor * values, values)


def shard_levels(rng, extent, pieces, least, high):
    def one(dim, parts):
        draws = jax.random.uniform(jax.random.fold_in(jax.random.fold_in(rng, 6), dim), (parts,), jnp.float32, least / len(pieces), high / len(pieces))
        return jnp.repeat(jnp.exp(draws), extent[dim] // parts).reshape((-1,) + (1,) * (len(extent) - dim - 1))

    gain = one(*pieces[0])
    for cut in pieces[1:]:
        gain = gain * one(*cut)
    return gain


def scatter_about(stream_key, extent, scale, bound, cuts=(), kind=jnp.bfloat16):
    factor_of = shard_levels(stream_key, extent, cuts, -0.22, 0.18) if cuts else 1.0
    drawn = jax.random.normal(stream_key, extent, jnp.float32) * scale * factor_of
    return jnp.minimum(jnp.maximum(drawn, -bound), bound).astype(kind)


def bell_draw_with(key, shape, scale, limit, shards, heavy, kind=jnp.bfloat16):
    values = scale * jax.random.normal(key, shape, jnp.float32)
    if shards:
        values = values * shard_levels(key, shape, shards, -0.22, 0.18)
    return jnp.clip(with_spikes(values, jax.random.fold_in(key, 3), *heavy), -limit, limit).astype(kind)


def setup_inputs(seed: int = 0) -> dict:
    key_of = jax.random.split(jax.random.key(seed), 6)
    features = scatter_about(key_of[0], (3, TOKENS, D), 1.0, 6.0, ((1, 16), (2, 2)))
    short_filter = scatter_about(key_of[1], (3, KERNEL, D), KERNEL ** -0.5, 2.0, ((2, 2),), jnp.float32)
    residues = scatter_about(key_of[2], (D, MODES), 0.25, 1.5, ((0, 2),), jnp.float32)
    rates = draw_rates(jax.random.fold_in(key_of[5], 71), 0)
    out_weight = bell_draw_with(key_of[4], (D, D), D ** -0.5, 0.125, ((0, 16), (1, 2)), (0, 1, 16, 2.0))
    return dict(features=features, short_filter=short_filter, residues=residues, rates=rates, out_weight=out_weight)


def short_conv(extended, taps, length):
    width = taps.shape[1]
    running = jnp.zeros((extended.shape[0], length, extended.shape[2]), jnp.float32)
    for offset in range(width):
        window = extended[:, width - 1 - offset:width - 1 - offset + length, :].astype(jnp.float32)
        running = running + taps[:, offset, None, :] * window
    return running

def reference(features, short_filter, residues, rates, out_weight):
    width = short_filter.shape[1]
    block_width = 128 if D % 128 == 0 else D
    groups = D // block_width
    count = TOKENS // BLOCK
    positions = jnp.arange(BLOCK, dtype=jnp.float32)
    lag_table = jnp.arange(BLOCK, dtype=jnp.int32)[:, None] - jnp.arange(BLOCK, dtype=jnp.int32)[None, :]
    causal = lag_table >= 0
    clipped = jnp.maximum(lag_table, 0)

    def one_group(packed):
        stream, taps, group_residues, group_rates = packed
        padded = jnp.pad(stream, ((0, 0), (width - 1, 0), (0, 0)))
        featured = short_conv(padded, taps, TOKENS)
        gated = (featured[1] * featured[2]).astype(jnp.bfloat16)
        scaled = group_residues * jnp.sqrt(-jnp.expm1(-2.0 * group_rates))
        decays = jnp.exp(-group_rates[:, :, None] * positions[None, None, :])
        lag_filter = jnp.einsum('cn,cnl->cl', scaled, decays, precision=lax.Precision.HIGHEST)
        toeplitz = jnp.where(causal[None], lag_filter[:, clipped], jnp.float32(0.0))
        blocks = gated.reshape(count, BLOCK, block_width).astype(jnp.float32)
        local = jnp.einsum('cij,bjc->bic', toeplitz, blocks, precision=lax.Precision.HIGHEST)
        end_weights = jnp.exp(-group_rates[None] * (BLOCK - positions)[:, None, None])
        start_weights = jnp.exp(-group_rates[None] * positions[:, None, None]) * scaled[None]
        block_states = jnp.einsum('bjc,jcn->bcn', blocks, end_weights, precision=lax.Precision.HIGHEST)
        step_decay = jnp.exp(-group_rates * BLOCK)

        def advance(carried, state):
            return (step_decay * carried + state, carried)
        _, carried_all = lax.scan(advance, jnp.zeros_like(step_decay), block_states)
        far_term = jnp.einsum('icn,bcn->bic', start_weights, carried_all, precision=lax.Precision.HIGHEST)
        long_rows = (local + far_term).reshape(TOKENS, block_width)
        return (featured[0] * long_rows).astype(jnp.bfloat16)
    streams = jnp.moveaxis(features.reshape(3, TOKENS, groups, block_width), 2, 0)
    taps_all = jnp.moveaxis(short_filter.reshape(3, width, groups, block_width), 2, 0)
    outputs = lax.map(one_group, (streams, taps_all, residues.reshape(groups, block_width, MODES), rates.reshape(groups, block_width, MODES)))
    combined = jnp.moveaxis(outputs, 0, 1).reshape(TOKENS, D)
    return jnp.dot(combined, out_weight, preferred_element_type=jnp.float32).astype(jnp.bfloat16)
```

```python
import jax
import jax.numpy as jnp
from jax import lax
from jax.experimental import pallas as pl
from jax.experimental.pallas import tpu as pltpu
from jax.sharding import PartitionSpec as P

LANES = 128
ROWS = 8
STEP = 8


def shifted(block, axis, distance):
    devices = range(lax.axis_size(axis))
    route = [(i - distance, i) for i in devices if i - distance in devices]
    return lax.ppermute(block, axis, route)


def scan_kernel(feat, halo, taps, decay, seg_decay, gated, fq, inclusive, ext):
    length = feat.shape[1]
    width = taps.shape[1]
    modes = decay.shape[0]
    seg = length // ROWS
    for r in range(3):
        ext[r, ROWS:, :] = feat[r].astype(jnp.float32)
        ext[r, ROWS - (width - 1) : ROWS, :] = halo[r].astype(jnp.float32)
    shape = (ROWS, LANES)
    tap = [[jnp.broadcast_to(taps[r, j : j + 1, :], shape) for j in range(width)] for r in range(3)]

    @pl.loop(0, seg // STEP)
    def _(block):
        start = block * STEP
        out = []
        for r in range(3):
            rows = [
                ext[r, pl.ds(start + i + ROWS - (width - 1), ROWS, stride=seg), :]
                for i in range(STEP + width - 1)
            ]
            out.append(
                [
                    sum(
                        (tap[r][j] * rows[i + width - 1 - j] for j in range(1, width)),
                        tap[r][0] * rows[i + width - 1],
                    )
                    for i in range(STEP)
                ]
            )
        for i in range(STEP):
            fq[start + i] = out[0][i]
            gated[start + i] = (out[1][i] * out[2][i]).astype(jnp.bfloat16).astype(jnp.float32)

    step_decay = [jnp.broadcast_to(decay[n : n + 1, :], shape) for n in range(modes)]

    def advance(block, states):
        for i in range(STEP):
            g = gated[block * STEP + i]
            states = tuple(d * s + g for d, s in zip(step_decay, states))
        return states

    states = lax.fori_loop(0, seg // STEP, advance, (jnp.zeros(shape, jnp.float32),) * modes)
    row = lax.broadcasted_iota(jnp.int32, shape, 0)
    for n in range(modes):
        value = states[n]
        factor = jnp.broadcast_to(seg_decay[n : n + 1, :], shape)
        distance = 1
        while distance < ROWS:
            value = value + jnp.where(row >= distance, factor * pltpu.roll(value, distance, 0), 0.0)
            factor = factor * factor
            distance *= 2
        inclusive[n] = value


def mix_kernel(gated, fq, inclusive, carried, rates, decay, scaled, combined, rows_out):
    seg = gated.shape[0]
    modes = decay.shape[0]
    shape = (ROWS, LANES)
    row = lax.broadcasted_iota(jnp.int32, shape, 0)
    offset = (row * seg).astype(jnp.float32)
    starts = []
    for n in range(modes):
        before = jnp.where(row == 0, 0.0, pltpu.roll(inclusive[n], 1, 0))
        starts.append(before + jnp.exp(-rates[n : n + 1, :] * offset) * carried[n : n + 1, :])
    step_decay = [jnp.broadcast_to(decay[n : n + 1, :], shape) for n in range(modes)]
    weight = [jnp.broadcast_to(scaled[n : n + 1, :], shape) for n in range(modes)]

    def advance(block, states):
        for i in range(STEP):
            t = block * STEP + i
            g = gated[t]
            states = tuple(d * s + g for d, s in zip(step_decay, states))
            terms = [w * s for w, s in zip(weight, states)]
            while len(terms) > 1:
                terms = [sum(terms[k + 1 : k + 2], terms[k]) for k in range(0, len(terms), 2)]
            rows_out[pl.ds(t, ROWS, stride=seg), :] = fq[t] * terms[0]
        return states

    lax.fori_loop(0, seg // STEP, advance, tuple(starts))
    combined[...] = rows_out[...].astype(jnp.bfloat16)


def columns(*lead):
    return pl.BlockSpec(lead + (LANES,), lambda c: (0,) * len(lead) + (c,))


def local_scan(features, halo, taps, decay, seg_decay):
    _, length, channels = features.shape
    width = taps.shape[1]
    modes = decay.shape[0]
    seg = length // ROWS
    f32 = jnp.float32
    return pl.pallas_call(
        scan_kernel,
        grid=(channels // LANES,),
        in_specs=[
            columns(3, length),
            columns(3, width - 1),
            columns(3, width),
            columns(modes),
            columns(modes),
        ],
        out_specs=[columns(seg, ROWS), columns(seg, ROWS), columns(modes, ROWS)],
        out_shape=[
            jax.ShapeDtypeStruct((seg, ROWS, channels), f32),
            jax.ShapeDtypeStruct((seg, ROWS, channels), f32),
            jax.ShapeDtypeStruct((modes, ROWS, channels), f32),
        ],
        scratch_shapes=[pltpu.VMEM((3, length + ROWS, LANES), f32)],
        compiler_params=pltpu.CompilerParams(vmem_limit_bytes=16 << 20),
        cost_estimate=pl.CostEstimate(
            flops=length * channels * (42 + 2 * modes),
            bytes_accessed=length * channels * 14,
            transcendentals=0,
        ),
        name="local_scan",
    )(features, halo, taps, decay, seg_decay)


def mix(gated, fq, inclusive, carried, rates, decay, scaled):
    seg, _, channels = gated.shape
    modes = rates.shape[0]
    length = seg * ROWS
    return pl.pallas_call(
        mix_kernel,
        grid=(channels // LANES,),
        in_specs=[columns(seg, ROWS), columns(seg, ROWS), columns(modes, ROWS)] + [columns(modes)] * 4,
        out_specs=columns(length),
        out_shape=jax.ShapeDtypeStruct((length, channels), jnp.bfloat16),
        scratch_shapes=[pltpu.VMEM((length, LANES), jnp.float32)],
        compiler_params=pltpu.CompilerParams(vmem_limit_bytes=16 << 20),
        cost_estimate=pl.CostEstimate(
            flops=length * channels * 4 * modes,
            bytes_accessed=length * channels * 10,
            transcendentals=0,
        ),
        name="mix",
    )(gated, fq, inclusive, carried, rates, decay, scaled)


def carried_state(own, rates, length):
    state = shifted(own, "ctx", 1)
    distance = 1
    while distance < lax.axis_size("ctx"):
        state = state + jnp.exp(-rates * (length * distance)) * shifted(state, "ctx", distance)
        distance *= 2
    return state


def body(features, short_filter, residues, rates, out_weight):
    length, channels = features.shape[1:]
    width = short_filter.shape[1]
    weights = lax.all_gather(out_weight, "ctx", axis=0, tiled=True)
    halo = shifted(features[:, length - (width - 1) :, :], "ctx", 1)
    scaled = (residues * jnp.sqrt(-jnp.expm1(-2.0 * rates))).T
    rates = rates.T
    decay = jnp.exp(-rates)
    gated, fq, inclusive = local_scan(
        features, halo, short_filter, decay, jnp.exp(-rates * (length // ROWS))
    )
    carried = carried_state(inclusive[:, ROWS - 1, :], rates, length)
    combined = mix(gated, fq, inclusive, carried, rates, decay, scaled)
    count, mine = lax.axis_size("mp"), lax.axis_index("mp")
    gathered = jnp.zeros((length, count * channels), jnp.bfloat16)
    for hop in range(count):
        if hop:
            ring = [(i, (i + 1) % count) for i in range(count)]
            combined = lax.ppermute(combined, "mp", ring)
        owner = lax.rem(mine + count - hop, count)
        gathered = lax.dynamic_update_slice(gathered, combined, (0, owner * channels))
    result = jnp.dot(gathered, weights, preferred_element_type=jnp.float32)
    return result.astype(jnp.bfloat16)


def solution(mesh):
    placed = (
        P(None, "ctx", "mp"),
        P(None, None, "mp"),
        P("mp", None),
        P("mp", None),
        P("ctx", "mp"),
    )
    return jax.shard_map(
        body, mesh=mesh, in_specs=placed, out_specs=P("ctx", "mp"), check_vma=False
    )
```

```python
import jax
import jax.numpy as jnp
from jax import lax
from jax.experimental import pallas as pl
from jax.experimental.pallas import tpu as pltpu
from jax.sharding import PartitionSpec as P

LANES = 128
ROWS = 8
STEP = 8
HALO = 16
F32 = jnp.float32
MESH = pl.DeviceIdType.MESH


def mixer_kernel(n, m, feat, taps, decay, seg_decay, rates, scaled, own_weight, out,
                 halo, ext, gated, fq, inclusive, states, arrived, weight, combined, total,
                 w_send, w_recv, s_send, s_recv, x_send, x_recv, h_send, h_recv, local_sem):
    length, channels = feat.shape[1:]
    width = taps.shape[1]
    modes = decay.shape[0]
    depth, wide = own_weight.shape
    seg = length // ROWS
    blocks = channels // LANES
    chips = n // 2
    side = 2 if chips % 2 == 0 else 1
    line = chips // side
    me, mine = lax.axis_index("ctx"), lax.axis_index("mp")
    core = lax.rem(me, 2)
    chip = lax.div(me, 2)
    b = lax.rem(chip, side)
    a = lax.div(chip, side)
    partner = me + 1 - 2 * core
    across = me + 2 * (1 - 2 * b)
    jump = 2 * side
    distances = [1 << k for k in range(n.bit_length()) if (1 << k) < n]

    barrier = pltpu.get_barrier_semaphore()
    for d in distances:
        for sign in (1, -1):
            other = me + sign * d

            @pl.when((other >= 0) & (other < n))
            def _():
                pl.semaphore_signal(barrier, inc=1, device_id={"ctx": other}, device_id_type=MESH)

    for k in range(1, m):
        pl.semaphore_signal(
            barrier, inc=1, device_id={"mp": lax.rem(mine + k, m)}, device_id_type=MESH
        )
    peers = m - 1
    for d in distances:
        peers = peers + (me >= d).astype(jnp.int32) + (me + d < n).astype(jnp.int32)
    pl.semaphore_wait(barrier, peers)

    def slot(s):
        return weight.at[pl.ds(pl.multiple_of(s * depth, depth), depth), :]

    def push(kind, s, to, source=None):
        return pltpu.make_async_remote_copy(
            src_ref=slot(s) if source is None else source,
            dst_ref=slot(s),
            send_sem=w_send.at[kind, s],
            recv_sem=w_recv.at[s],
            device_id={"ctx": to},
            device_id_type=MESH,
        )

    def halo_copy():
        return pltpu.make_async_remote_copy(
            src_ref=feat.at[:, length - HALO :, :],
            dst_ref=halo,
            send_sem=h_send,
            recv_sem=h_recv,
            device_id={"ctx": lax.rem(me + 1, n)},
            device_id_type=MESH,
        )

    up, down = a < line - 1, a > 0

    @pl.when(me < n - 1)
    def _():
        halo_copy().start()

    @pl.when(up)
    def _():
        push(0, me, me + jump, own_weight).start()

    @pl.when(down)
    def _():
        push(1, me, me - jump, own_weight).start()

    if side == 2:
        push(2, me, across, own_weight).start()
    push(3, me, partner, own_weight).start()
    keep = pltpu.make_async_copy(own_weight, slot(me), local_sem)
    keep.start()

    @pl.when(me > 0)
    def _():
        halo_copy().wait_recv()

    @pl.when(me == 0)
    def _():
        halo[...] = jnp.zeros_like(halo)

    shape = (ROWS, LANES)
    row = lax.broadcasted_iota(jnp.int32, shape, 0)

    @pl.loop(0, blocks)
    def _(c):
        cols = pl.ds(pl.multiple_of(c * LANES, LANES), LANES)
        for r in range(3):
            ext[r, ROWS:, :] = feat[r, :, cols].astype(F32)
            ext[r, :ROWS, :] = halo[r, :, cols].astype(F32)[HALO - ROWS :, :]
        tap = [
            [jnp.broadcast_to(taps[r, j : j + 1, cols], shape) for j in range(width)]
            for r in range(3)
        ]

        @pl.loop(0, seg // STEP)
        def _(block):
            start = block * STEP
            made = []
            for r in range(3):
                rows = [
                    ext[r, pl.ds(start + i + ROWS - (width - 1), ROWS, stride=seg), :]
                    for i in range(STEP + width - 1)
                ]
                made.append(
                    [
                        sum(
                            (tap[r][j] * rows[i + width - 1 - j] for j in range(1, width)),
                            tap[r][0] * rows[i + width - 1],
                        )
                        for i in range(STEP)
                    ]
                )
            for i in range(STEP):
                at = c * seg + start + i
                fq[at] = made[0][i]
                gated[at] = (made[1][i] * made[2][i]).astype(jnp.bfloat16).astype(F32)

        step_decay = [jnp.broadcast_to(decay[k : k + 1, cols], shape) for k in range(modes)]

        def advance(block, modal):
            for i in range(STEP):
                g = gated[c * seg + block * STEP + i]
                modal = tuple(d * s + g for d, s in zip(step_decay, modal))
            return modal

        modal = lax.fori_loop(0, seg // STEP, advance, (jnp.zeros(shape, F32),) * modes)
        for k in range(modes):
            value = modal[k]
            factor = jnp.broadcast_to(seg_decay[k : k + 1, cols], shape)
            distance = 1
            while distance < ROWS:
                earlier = pltpu.roll(value, distance, 0)
                value = value + jnp.where(row >= distance, factor * earlier, 0.0)
                factor = factor * factor
                distance *= 2
            inclusive[c * modes + k] = value
            states[0, k : k + 1, cols] = value[ROWS - 1 :, :]

    hops = [1] + distances
    for level, d in enumerate(hops):
        def hop_copy(level=level, d=d):
            return pltpu.make_async_remote_copy(
                src_ref=states.at[level],
                dst_ref=arrived.at[level],
                send_sem=s_send.at[level],
                recv_sem=s_recv.at[level],
                device_id={"ctx": lax.rem(me + d, n)},
                device_id_type=MESH,
            )

        @pl.when(me + d < n)
        def _():
            hop_copy().start()

        @pl.when(me >= d)
        def _():
            hop_copy().wait_recv()
            if level == 0:
                states[1] = arrived[0]
            else:
                states[level + 1] = states[level] + jnp.exp(rates[...] * (-1.0 * length * d)) * arrived[level]

        @pl.when(me < d)
        def _():
            states[level + 1] = jnp.zeros_like(states[1]) if level == 0 else states[level]

    carried = len(hops)

    def take(s):
        push(3, s, partner).wait_recv()

    def serve_line(k):
        @pl.when(a >= k)
        def _():
            s = me - k * jump
            take(s)
            if side == 2:
                push(2, s, across).start()

            @pl.when(up)
            def _():
                push(0, s, me + jump).start()

            push(3, s, partner).start()

        @pl.when(a + k < line)
        def _():
            s = me + k * jump
            take(s)
            if side == 2:
                push(2, s, across).start()

            @pl.when(down)
            def _():
                push(1, s, me - jump).start()

            push(3, s, partner).start()

    def serve_side(k):
        if side == 2:
            for sign in (1, -1) if k else (1,):
                @pl.when((a + sign * k >= 0) & (a + sign * k < line))
                def _():
                    s = across + sign * k * jump
                    take(s)
                    push(3, s, partner).start()

    if line > 1:
        serve_line(1)
    serve_side(0)

    parts = x_recv.shape[1]
    part = channels // parts

    def swap(k, p):
        where = combined.at[mine, :, pl.ds(pl.multiple_of(p * part, part), part)]
        return pltpu.make_async_remote_copy(
            src_ref=where,
            dst_ref=where,
            send_sem=x_send.at[k, p],
            recv_sem=x_recv.at[mine, p],
            device_id={"mp": lax.rem(mine + k, m)},
            device_id_type=MESH,
        )

    offset = (row * seg).astype(F32)

    @pl.loop(0, parts)
    def _(p):
        @pl.loop(0, blocks // parts)
        def _(q):
            c = p * (blocks // parts) + q
            cols = pl.ds(pl.multiple_of(c * LANES, LANES), LANES)
            starts = []
            for k in range(modes):
                before = jnp.where(row == 0, 0.0, pltpu.roll(inclusive[c * modes + k], 1, 0))
                fade = jnp.exp(-rates[k : k + 1, cols] * offset)
                starts.append(before + fade * states[carried, k : k + 1, cols])
            step_decay = [jnp.broadcast_to(decay[k : k + 1, cols], shape) for k in range(modes)]
            gain = [jnp.broadcast_to(scaled[k : k + 1, cols], shape) for k in range(modes)]

            def advance(block, modal):
                for i in range(STEP):
                    t = block * STEP + i
                    g = gated[c * seg + t]
                    modal = tuple(d * s + g for d, s in zip(step_decay, modal))
                    terms = [w * s for w, s in zip(gain, modal)]
                    while len(terms) > 1:
                        terms = [sum(terms[k + 1 : k + 2], terms[k]) for k in range(0, len(terms), 2)]
                    ext[0, pl.ds(t, ROWS, stride=seg), :] = fq[c * seg + t] * terms[0]
                return modal

            lax.fori_loop(0, seg // STEP, advance, tuple(starts))
            combined[mine, :, cols] = ext[0, :length, :].astype(jnp.bfloat16)

        for k in range(1, m):
            swap(k, p).start()

    for k in range(2, line):
        serve_line(k)
        serve_side(k - 1)

    for k in range(max(line - 1, 1), line):
        serve_side(k)

    keep.wait()

    tile = 256 if wide % 256 == 0 else wide
    per_group = chips // m

    def multiply(group, first):
        def one(k, h):
            aa = lax.div(group * per_group, side) + k
            bb = lax.rem(b + h, side)
            which = aa * side + bb
            take(which * 2 + 1 - core)
            rows = pl.ds(pl.multiple_of(which * 2 * depth, 2 * depth), 2 * depth)
            take_cols = pl.ds(
                pl.multiple_of((which - group * per_group) * 2 * depth, 2 * depth), 2 * depth
            )

            @pl.loop(0, wide // tile)
            def _(j):
                cols = pl.ds(pl.multiple_of(j * tile, tile), tile)
                product = jnp.dot(
                    combined[group, :, take_cols], weight[rows, cols], preferred_element_type=F32
                )
                if first and h == 0:
                    @pl.when(k == 0)
                    def _():
                        total[:, cols] = product

                    @pl.when(k > 0)
                    def _():
                        total[:, cols] += product
                else:
                    total[:, cols] += product

        for h in range(side):
            @pl.loop(0, per_group // side)
            def _(k, h=h):
                one(k, h)

    multiply(mine, True)
    for k in range(1, m):
        group = lax.rem(mine + k, m)
        for p in range(parts):
            where = combined.at[group, :, p * part : (p + 1) * part]
            pltpu.make_async_remote_copy(
                src_ref=where,
                dst_ref=where,
                send_sem=x_send.at[k, p],
                recv_sem=x_recv.at[group, p],
                device_id={"mp": group},
                device_id_type=MESH,
            ).wait_recv()
        multiply(group, False)

    out[...] = total[...].astype(out.dtype)

    @pl.when(me < n - 1)
    def _():
        halo_copy().wait_send()

    for level, d in enumerate(hops):
        @pl.when(me + d < n)
        def _(level=level, d=d):
            pltpu.make_async_remote_copy(
                src_ref=states.at[level],
                dst_ref=arrived.at[level],
                send_sem=s_send.at[level],
                recv_sem=s_recv.at[level],
                device_id={"ctx": lax.rem(me + d, n)},
                device_id_type=MESH,
            ).wait_send()

    for k in range(1, m):
        for p in range(parts):
            swap(k, p).wait_send()

    @pl.loop(0, line)
    def _(aa):
        s = (aa * side + b) * 2 + core

        @pl.when(up & (aa <= a))
        def _():
            push(0, s, me + jump).wait_send()

        @pl.when(down & (aa >= a))
        def _():
            push(1, s, me - jump).wait_send()

        if side == 2:
            push(2, s, across).wait_send()

    @pl.loop(0, chips)
    def _(which):
        push(3, which * 2 + core, partner).wait_send()


def mixer(features, taps, decay, seg_decay, rates, scaled, own_weight):
    n, m = lax.axis_size("ctx"), lax.axis_size("mp")
    length, channels = features.shape[1:]
    modes = rates.shape[0]
    depth, wide = own_weight.shape
    blocks = channels // LANES
    seg = length // ROWS
    levels = 1 + len([k for k in range(n.bit_length()) if (1 << k) < n])
    parts = 4 if blocks % 4 == 0 else 1
    dma = pltpu.SemaphoreType.DMA
    whole = pl.BlockSpec(memory_space=pltpu.VMEM)
    return pl.pallas_call(
        lambda *refs: mixer_kernel(n, m, *refs),
        out_shape=jax.ShapeDtypeStruct((length, wide), jnp.bfloat16),
        in_specs=[whole] * 7,
        out_specs=whole,
        scratch_shapes=[
            pltpu.VMEM((3, HALO, channels), jnp.bfloat16),
            pltpu.VMEM((3, length + ROWS, LANES), F32),
            pltpu.VMEM((blocks * seg, ROWS, LANES), F32),
            pltpu.VMEM((blocks * seg, ROWS, LANES), F32),
            pltpu.VMEM((blocks * modes, ROWS, LANES), F32),
            pltpu.VMEM((levels + 1, modes, channels), F32),
            pltpu.VMEM((levels, modes, channels), F32),
            pltpu.VMEM((n * depth, wide), jnp.bfloat16),
            pltpu.VMEM((m, length, channels), jnp.bfloat16),
            pltpu.VMEM((length, wide), F32),
            dma((4, n)),
            dma((n,)),
            dma((levels,)),
            dma((levels,)),
            dma((m, parts)),
            dma((m, parts)),
            dma,
            dma,
            dma,
        ],
        compiler_params=pltpu.CompilerParams(
            collective_id=0, has_side_effects=True, vmem_limit_bytes=58 << 20
        ),
        name="mixer",
    )(features, taps, decay, seg_decay, rates, scaled, own_weight)


def body(features, short_filter, residues, rates, out_weight):
    length = features.shape[1]
    scaled = (residues * jnp.sqrt(-jnp.expm1(-2.0 * rates))).T
    rates = rates.T
    decay = jnp.exp(-rates)
    seg_decay = jnp.exp(-rates * (length // ROWS))
    return mixer(features, short_filter, decay, seg_decay, rates, scaled, out_weight)


def solution(mesh):
    placed = (
        P(None, "ctx", "mp"),
        P(None, None, "mp"),
        P("mp", None),
        P("mp", None),
        P("ctx", "mp"),
    )
    return jax.shard_map(
        body, mesh=mesh, in_specs=placed, out_specs=P("ctx", "mp"), check_vma=False
    )
```

```python
import jax
import jax.numpy as jnp
from jax import lax
from jax.experimental import pallas as pl
from jax.experimental.pallas import tpu as pltpu
from jax.sharding import PartitionSpec as P

LANES = 128
ROWS = 8
STEP = 8
HALO = 16
F32 = jnp.float32
MESH = pl.DeviceIdType.MESH


def mixer_kernel(n, m, feat, taps, decay, seg_decay, rates, scaled, own_weight, out,
                 halo, ext, gated, fq, inclusive, states, arrived, weight, combined, total,
                 w_send, w_recv, s_send, s_recv, x_send, x_recv, h_send, h_recv, local_sem):
    length, channels = feat.shape[1:]
    width = taps.shape[1]
    modes = decay.shape[0]
    depth, wide = own_weight.shape
    seg = length // ROWS
    blocks = channels // LANES
    chips = n // 2
    side = 2 if chips % 2 == 0 else 1
    line = chips // side
    me, mine = lax.axis_index("ctx"), lax.axis_index("mp")
    core = lax.rem(me, 2)
    chip = lax.div(me, 2)
    b = lax.rem(chip, side)
    a = lax.div(chip, side)
    partner = me + 1 - 2 * core
    across = me + 2 * (1 - 2 * b)
    jump = 2 * side
    distances = [1 << k for k in range(n.bit_length()) if (1 << k) < n]

    barrier = pltpu.get_barrier_semaphore()
    for d in distances:
        for sign in (1, -1):
            other = me + sign * d

            @pl.when((other >= 0) & (other < n))
            def _():
                pl.semaphore_signal(barrier, inc=1, device_id={"ctx": other}, device_id_type=MESH)

    for k in range(1, m):
        pl.semaphore_signal(
            barrier, inc=1, device_id={"mp": lax.rem(mine + k, m)}, device_id_type=MESH
        )
    peers = m - 1
    for d in distances:
        peers = peers + (me >= d).astype(jnp.int32) + (me + d < n).astype(jnp.int32)
    pl.semaphore_wait(barrier, peers)

    def slot(s):
        return weight.at[pl.ds(pl.multiple_of(s * depth, depth), depth), :]

    def push(kind, s, to, source=None):
        return pltpu.make_async_remote_copy(
            src_ref=slot(s) if source is None else source,
            dst_ref=slot(s),
            send_sem=w_send.at[kind, s],
            recv_sem=w_recv.at[s],
            device_id={"ctx": to},
            device_id_type=MESH,
        )

    def halo_copy():
        return pltpu.make_async_remote_copy(
            src_ref=feat.at[:, length - HALO :, :],
            dst_ref=halo,
            send_sem=h_send,
            recv_sem=h_recv,
            device_id={"ctx": lax.rem(me + 1, n)},
            device_id_type=MESH,
        )

    up, down = a < line - 1, a > 0

    @pl.when(me < n - 1)
    def _():
        halo_copy().start()

    @pl.when(up)
    def _():
        push(0, me, me + jump, own_weight).start()

    @pl.when(down)
    def _():
        push(1, me, me - jump, own_weight).start()

    if side == 2:
        push(2, me, across, own_weight).start()
    push(3, me, partner, own_weight).start()
    keep = pltpu.make_async_copy(own_weight, slot(me), local_sem)
    keep.start()

    @pl.when(me > 0)
    def _():
        halo_copy().wait_recv()

    @pl.when(me == 0)
    def _():
        halo[...] = jnp.zeros_like(halo)

    shape = (ROWS, LANES)
    row = lax.broadcasted_iota(jnp.int32, shape, 0)

    @pl.loop(0, blocks)
    def _(c):
        cols = pl.ds(pl.multiple_of(c * LANES, LANES), LANES)
        for r in range(3):
            ext[r, ROWS:, :] = feat[r, :, cols].astype(F32)
            ext[r, :ROWS, :] = halo[r, :, cols].astype(F32)[HALO - ROWS :, :]
        tap = [
            [jnp.broadcast_to(taps[r, j : j + 1, cols], shape) for j in range(width)]
            for r in range(3)
        ]

        @pl.loop(0, seg // STEP)
        def _(block):
            start = block * STEP
            made = []
            for r in range(3):
                rows = [
                    ext[r, pl.ds(start + i + ROWS - (width - 1), ROWS, stride=seg), :]
                    for i in range(STEP + width - 1)
                ]
                made.append(
                    [
                        sum(
                            (tap[r][j] * rows[i + width - 1 - j] for j in range(1, width)),
                            tap[r][0] * rows[i + width - 1],
                        )
                        for i in range(STEP)
                    ]
                )
            for i in range(STEP):
                at = c * seg + start + i
                fq[at] = made[0][i]
                gated[at] = (made[1][i] * made[2][i]).astype(jnp.bfloat16).astype(F32)

        step_decay = [jnp.broadcast_to(decay[k : k + 1, cols], shape) for k in range(modes)]

        def advance(block, modal):
            for i in range(STEP):
                g = gated[c * seg + block * STEP + i]
                modal = tuple(d * s + g for d, s in zip(step_decay, modal))
            return modal

        modal = lax.fori_loop(0, seg // STEP, advance, (jnp.zeros(shape, F32),) * modes)
        for k in range(modes):
            value = modal[k]
            factor = jnp.broadcast_to(seg_decay[k : k + 1, cols], shape)
            distance = 1
            while distance < ROWS:
                earlier = pltpu.roll(value, distance, 0)
                value = value + jnp.where(row >= distance, factor * earlier, 0.0)
                factor = factor * factor
                distance *= 2
            inclusive[c * modes + k] = value
            states[0, k : k + 1, cols] = value[ROWS - 1 :, :]

    hops = [1] + distances
    for level, d in enumerate(hops):
        def hop_copy(level=level, d=d):
            return pltpu.make_async_remote_copy(
                src_ref=states.at[level],
                dst_ref=arrived.at[level],
                send_sem=s_send.at[level],
                recv_sem=s_recv.at[level],
                device_id={"ctx": lax.rem(me + d, n)},
                device_id_type=MESH,
            )

        @pl.when(me + d < n)
        def _():
            hop_copy().start()

        @pl.when(me >= d)
        def _():
            hop_copy().wait_recv()
            if level == 0:
                states[1] = arrived[0]
            else:
                states[level + 1] = states[level] + jnp.exp(rates[...] * (-1.0 * length * d)) * arrived[level]

        @pl.when(me < d)
        def _():
            states[level + 1] = jnp.zeros_like(states[1]) if level == 0 else states[level]

    carried = len(hops)

    def take(s):
        push(3, s, partner).wait_recv()

    def serve_line(k):
        @pl.when(a >= k)
        def _():
            s = me - k * jump
            take(s)
            if side == 2:
                push(2, s, across).start()

            @pl.when(up)
            def _():
                push(0, s, me + jump).start()

            push(3, s, partner).start()

        @pl.when(a + k < line)
        def _():
            s = me + k * jump
            take(s)
            if side == 2:
                push(2, s, across).start()

            @pl.when(down)
            def _():
                push(1, s, me - jump).start()

            push(3, s, partner).start()

    def serve_side(k):
        if side == 2:
            for sign in (1, -1) if k else (1,):
                @pl.when((a + sign * k >= 0) & (a + sign * k < line))
                def _():
                    s = across + sign * k * jump
                    take(s)
                    push(3, s, partner).start()

    if line > 1:
        serve_line(1)
    serve_side(0)

    parts = x_recv.shape[1]
    part = channels // parts

    def swap(k, p):
        where = combined.at[mine, :, pl.ds(pl.multiple_of(p * part, part), part)]
        return pltpu.make_async_remote_copy(
            src_ref=where,
            dst_ref=where,
            send_sem=x_send.at[k, p],
            recv_sem=x_recv.at[mine, p],
            device_id={"mp": lax.rem(mine + k, m)},
            device_id_type=MESH,
        )

    offset = (row * seg).astype(F32)

    @pl.loop(0, parts)
    def _(p):
        @pl.loop(0, blocks // parts)
        def _(q):
            c = p * (blocks // parts) + q
            cols = pl.ds(pl.multiple_of(c * LANES, LANES), LANES)
            starts = []
            for k in range(modes):
                before = jnp.where(row == 0, 0.0, pltpu.roll(inclusive[c * modes + k], 1, 0))
                fade = jnp.exp(-rates[k : k + 1, cols] * offset)
                starts.append(before + fade * states[carried, k : k + 1, cols])
            step_decay = [jnp.broadcast_to(decay[k : k + 1, cols], shape) for k in range(modes)]
            gain = [jnp.broadcast_to(scaled[k : k + 1, cols], shape) for k in range(modes)]

            def advance(block, modal):
                for i in range(STEP):
                    t = block * STEP + i
                    g = gated[c * seg + t]
                    modal = tuple(d * s + g for d, s in zip(step_decay, modal))
                    terms = [w * s for w, s in zip(gain, modal)]
                    while len(terms) > 1:
                        terms = [sum(terms[k + 1 : k + 2], terms[k]) for k in range(0, len(terms), 2)]
                    ext[0, pl.ds(t, ROWS, stride=seg), :] = fq[c * seg + t] * terms[0]
                return modal

            lax.fori_loop(0, seg // STEP, advance, tuple(starts))
            combined[mine, :, cols] = ext[0, :length, :].astype(jnp.bfloat16)

        for k in range(1, m):
            swap(k, p).start()

    for k in range(2, line):
        serve_line(k)
        if k == 2:
            serve_side(1)

    if line == 2:
        serve_side(1)
    keep.wait()
    for k in range(1, m):
        group = lax.rem(mine + k, m)
        for p in range(parts):
            where = combined.at[group, :, p * part : (p + 1) * part]
            pltpu.make_async_remote_copy(
                src_ref=where,
                dst_ref=where,
                send_sem=x_send.at[k, p],
                recv_sem=x_recv.at[group, p],
                device_id={"mp": group},
                device_id_type=MESH,
            ).wait_recv()

    tile = 256 if wide % 256 == 0 else wide
    per_group = chips // m

    def multiply(aa, bb, first=False):
        which = aa * side + bb
        take(which * 2 + 1 - core)
        group = lax.div(which, per_group)
        rows = pl.ds(pl.multiple_of(which * 2 * depth, 2 * depth), 2 * depth)
        inner = pl.ds(
            pl.multiple_of((which - group * per_group) * 2 * depth, 2 * depth), 2 * depth
        )

        @pl.loop(0, wide // tile)
        def _(j):
            cols = pl.ds(pl.multiple_of(j * tile, tile), tile)
            product = jnp.dot(
                combined[group, :, inner], weight[rows, cols], preferred_element_type=F32
            )
            total[:, cols] = product if first else total[:, cols] + product

    def multiply_at(k, bb):
        for sign in (1, -1) if k else (1,):
            @pl.when((a + sign * k >= 0) & (a + sign * k < line))
            def _():
                multiply(a + sign * k, bb)

    multiply(a, b, first=True)
    for k in range(1, line):
        multiply_at(k, b)
    if side == 2:
        for k in range(line):
            if k >= 2:
                serve_side(k)
            multiply_at(k, 1 - b)

    out[...] = total[...].astype(out.dtype)

    @pl.when(me < n - 1)
    def _():
        halo_copy().wait_send()

    for level, d in enumerate(hops):
        @pl.when(me + d < n)
        def _(level=level, d=d):
            pltpu.make_async_remote_copy(
                src_ref=states.at[level],
                dst_ref=arrived.at[level],
                send_sem=s_send.at[level],
                recv_sem=s_recv.at[level],
                device_id={"ctx": lax.rem(me + d, n)},
                device_id_type=MESH,
            ).wait_send()

    for k in range(1, m):
        for p in range(parts):
            swap(k, p).wait_send()

    @pl.loop(0, line)
    def _(aa):
        s = (aa * side + b) * 2 + core

        @pl.when(up & (aa <= a))
        def _():
            push(0, s, me + jump).wait_send()

        @pl.when(down & (aa >= a))
        def _():
            push(1, s, me - jump).wait_send()

        if side == 2:
            push(2, s, across).wait_send()

    @pl.loop(0, chips)
    def _(which):
        push(3, which * 2 + core, partner).wait_send()


def mixer(features, taps, decay, seg_decay, rates, scaled, own_weight):
    n, m = lax.axis_size("ctx"), lax.axis_size("mp")
    length, channels = features.shape[1:]
    modes = rates.shape[0]
    depth, wide = own_weight.shape
    blocks = channels // LANES
    seg = length // ROWS
    levels = 1 + len([k for k in range(n.bit_length()) if (1 << k) < n])
    parts = 4 if blocks % 4 == 0 else 1
    dma = pltpu.SemaphoreType.DMA
    whole = pl.BlockSpec(memory_space=pltpu.VMEM)
    return pl.pallas_call(
        lambda *refs: mixer_kernel(n, m, *refs),
        out_shape=jax.ShapeDtypeStruct((length, wide), jnp.bfloat16),
        in_specs=[whole] * 7,
        out_specs=whole,
        scratch_shapes=[
            pltpu.VMEM((3, HALO, channels), jnp.bfloat16),
            pltpu.VMEM((3, length + ROWS, LANES), F32),
            pltpu.VMEM((blocks * seg, ROWS, LANES), F32),
            pltpu.VMEM((blocks * seg, ROWS, LANES), F32),
            pltpu.VMEM((blocks * modes, ROWS, LANES), F32),
            pltpu.VMEM((levels + 1, modes, channels), F32),
            pltpu.VMEM((levels, modes, channels), F32),
            pltpu.VMEM((n * depth, wide), jnp.bfloat16),
            pltpu.VMEM((m, length, channels), jnp.bfloat16),
            pltpu.VMEM((length, wide), F32),
            dma((4, n)),
            dma((n,)),
            dma((levels,)),
            dma((levels,)),
            dma((m, parts)),
            dma((m, parts)),
            dma,
            dma,
            dma,
        ],
        compiler_params=pltpu.CompilerParams(
            collective_id=0, has_side_effects=True, vmem_limit_bytes=58 << 20
        ),
        name="mixer",
    )(features, taps, decay, seg_decay, rates, scaled, own_weight)


def body(features, short_filter, residues, rates, out_weight):
    length = features.shape[1]
    scaled = (residues * jnp.sqrt(-jnp.expm1(-2.0 * rates))).T
    rates = rates.T
    decay = jnp.exp(-rates)
    seg_decay = jnp.exp(-rates * (length // ROWS))
    return mixer(features, short_filter, decay, seg_decay, rates, scaled, out_weight)


def solution(mesh):
    placed = (
        P(None, "ctx", "mp"),
        P(None, None, "mp"),
        P("mp", None),
        P("mp", None),
        P("ctx", "mp"),
    )
    return jax.shard_map(
        body, mesh=mesh, in_specs=placed, out_specs=P("ctx", "mp"), check_vma=False
    )
```
